32 devices in a mesh: row: 8 (over z, y), col: 4 (over x, core).
Axes of the slice: x: 2, y: 2, z: 4, core: 2. Of those that a mesh axis runs over, the one named last changes fastest.
Arguments:
- entries: int32 [32, 16, 128, 128], P('row', 'col'), may hold values from -2 to 2
- tile_cols: int32 [32, 16], P('row', 'col'), may hold values from 0 to 31
- block_now: int32 [32, 16384], P(None, ('col', 'row')), may hold values from 0 to 65520
- block_prev: int32 [32, 16384], P(None, ('col', 'row')), may hold values from 0 to 65520
- block_prev2: int32 [32, 16384], P(None, ('col', 'row')), may hold values from 0 to 65520
- gram_prev: int32 [32, 32], replicated, may hold values from 0 to 65520
- square_prev: int32 [32, 32], replicated, may hold values from 0 to 65520
- inverse_prev: int32 [32, 32], replicated, may hold values from 0 to 65520
- inverse_prev2: int32 [32, 32], replicated, may hold values from 0 to 65520
Outputs:
- next_block: float32 [32, 16384], P(None, ('col', 'row'))
- later_block: float32 [32, 16384], P(None, ('col', 'row'))
The draws below stay inside these ranges and needn't reach their ends.
Inputs may be any that keep to these rules, and one draw needn't show every extreme that they name: `tile_cols`: stored tiles that name the same tile column in one tile row add. `block_prev`: residues. `block_prev2`: residues. `gram_prev`: residues. `square_prev`: residues. `inverse_prev`: residues. `inverse_prev2`: residues.
All inputs are finite; a program needn't handle non-finite values.
Results may differ from the reference program's by a relative error of at most 0.0003.
Values sent between devices are 32-bit elements; how exact they have to be, the bound alone decides.
A program may use at most 64 MiB of HBM per device.

```python
import jax
import jax.numpy as jnp
from jax import lax

BLOCK = 32
TILE = 128
SLOTS = 4
TCOLS = 32
ORDER = 16384
TROWS_ALL = 32
SLOTS_ALL = 16
N_COL = 4


def with_ends(values, key, least, top_value):
    extent = values.shape
    index_at = [jax.random.randint(jax.random.fold_in(key, axis), (), 0, extent[axis]) for axis in range(len(extent))]
    values = values.at[tuple(index_at)].set(least)
    longest = extent.index(max(extent))
    index_at[longest] = (index_at[longest] + 1) % extent[longest]
    return values.at[tuple(index_at)].set(top_value)


def setup_inputs(seed: int = 0) -> dict:
    seeds = jax.random.split(jax.random.key(seed), 10)
    return {
        "entries": with_ends(jax.random.randint(seeds[0], (TROWS_ALL, SLOTS_ALL, TILE, TILE), -2, 3), jax.random.fold_in(seeds[0], 1), -2, 2).astype(jnp.int32),
        "tile_cols": with_ends(jax.random.randint(seeds[1], (TROWS_ALL, SLOTS_ALL), 0, TCOLS), jax.random.fold_in(seeds[1], 1), 0, TCOLS - 1).astype(jnp.int32),
        "block_now": with_ends(jax.random.randint(seeds[2], (BLOCK, ORDER), 0, 65521), jax.random.fold_in(seeds[2], 1), 0, 65520).astype(jnp.int32),
        "block_prev": with_ends(jax.random.randint(seeds[3], (BLOCK, ORDER), 0, 65521), jax.random.fold_in(seeds[3], 1), 0, 65520).astype(jnp.int32),
        "block_prev2": with_ends(jax.random.randint(seeds[4], (BLOCK, ORDER), 0, 65521), jax.random.fold_in(seeds[4], 1), 0, 65520).astype(jnp.int32),
        "gram_prev": with_ends(jax.random.randint(seeds[5], (BLOCK, BLOCK), 0, 65521), jax.random.fold_in(seeds[5], 1), 0, 65520).astype(jnp.int32),
        "square_prev": with_ends(jax.random.randint(seeds[6], (BLOCK, BLOCK), 0, 65521), jax.random.fold_in(seeds[6], 1), 0, 65520).astype(jnp.int32),
        "inverse_prev": with_ends(jax.random.randint(seeds[7], (BLOCK, BLOCK), 0, 65521), jax.random.fold_in(seeds[7], 1), 0, 65520).astype(jnp.int32),
        "inverse_prev2": with_ends(jax.random.randint(seeds[8], (BLOCK, BLOCK), 0, 65521), jax.random.fold_in(seeds[8], 1), 0, 65520).astype(jnp.int32),
    }


modulus = 65521.0


def residue(values):
    return jnp.mod(values, modulus)


def split_digits(values):
    top_part = jnp.floor(values / 256.0)
    return top_part, values - top_part * 256.0


def fold_digits(top_sum, low_sum):
    return residue(residue(residue(top_sum) * 256.0) + residue(low_sum))


def fold_three(upper_part, middle, lower_part):
    return residue(residue(residue(upper_part) * 15.0) + residue(residue(middle) * 256.0) + residue(lower_part))


def mulmod(left_side, right_side):
    top_part, low_part = split_digits(right_side)
    return fold_digits(left_side * top_part, left_side * low_part)


def exact_dot(left_side, right_side):
    return jnp.dot(left_side, right_side, precision=lax.Precision.HIGHEST, preferred_element_type=jnp.float32)


def small_product(left_side, right_side):
    left_top, left_low = split_digits(left_side)
    right_top, right_low = split_digits(right_side)
    return fold_three(exact_dot(left_top, right_top), exact_dot(left_top, right_low) + exact_dot(left_low, right_top), exact_dot(left_low, right_low))


def inverse_scalar(number):
    result = jnp.ones_like(number)
    square = number
    exponent = 65519
    for position in range(16):
        if (exponent >> position) & 1:
            result = mulmod(result, square)
        square = mulmod(square, square)
    return result


def inverse_matrix(matrix):
    matrix_order = matrix.shape[0]
    augmented = jnp.concatenate([matrix, jnp.eye(matrix_order, dtype=matrix.dtype)], axis=1)
    row_numbers = jnp.arange(matrix_order, dtype=jnp.int32)

    def eliminate(column, augmented):
        column = jnp.asarray(column).astype(jnp.int32)
        pivot_column = augmented[:, column]
        usable = (pivot_column != 0.0) & (row_numbers >= column)
        pivot_row_id = jnp.where(jnp.any(usable), jnp.argmax(usable).astype(jnp.int32), column)
        pivot_row = augmented[pivot_row_id]
        current_row = augmented[column]
        swapped = jnp.where((row_numbers == column)[:, None], pivot_row[None, :], jnp.where((row_numbers == pivot_row_id)[:, None], current_row[None, :], augmented))
        scaled = mulmod(pivot_row, inverse_scalar(pivot_row[column]))
        factors = jnp.where(row_numbers == column, 0.0, swapped[:, column])
        reduced = residue(swapped - mulmod(factors[:, None], scaled[None, :]) + modulus)
        return jnp.where((row_numbers == column)[:, None], scaled[None, :], reduced)

    augmented = lax.fori_loop(0, matrix_order, eliminate, augmented)
    return augmented[:, matrix_order:]


def coefficients(gram_now, square_now, inverse_now, inverse_prev, inverse_prev2, gram_old, square_old):
    identity = jnp.eye(gram_now.shape[0], dtype=gram_now.dtype)
    first = residue(identity - small_product(residue(square_now + gram_now), inverse_now) + modulus)
    second = residue(modulus - small_product(gram_now, inverse_prev))
    middle = residue(identity - small_product(inverse_prev, gram_old) + modulus)
    third = residue(modulus - small_product(small_product(residue(square_old + gram_old), middle), inverse_prev2))
    return jnp.concatenate([first, second, third], axis=1)


def combine_blocks(coeffs, stacked):
    coeff_top, coeff_low = split_digits(coeffs)
    stack_top, stack_low = split_digits(stacked)
    left_side = jnp.stack([coeff_top, coeff_low])
    right_side = jnp.stack([stack_top, stack_low])
    products = jnp.einsum('dab,ebn->dean', left_side, right_side, precision=lax.Precision.HIGHEST)
    return fold_three(products[0, 0], products[0, 1] + products[1, 0], products[1, 1])


def gram_whole(first, second):
    column_count = first.shape[1]
    group_width = min(column_count, 128)
    groups = column_count // group_width
    first_digits = jnp.stack(split_digits(first)).reshape(2, first.shape[0], groups, group_width)
    second_digits = jnp.stack(split_digits(second)).reshape(2, second.shape[0], groups, group_width)
    products = jnp.einsum('dagw,ecgw->gdeac', first_digits, second_digits, precision=lax.Precision.HIGHEST)
    per_group = fold_three(products[:, 0, 0], products[:, 0, 1] + products[:, 1, 0], products[:, 1, 1])
    top_part, low_part = split_digits(per_group)
    return fold_digits(jnp.sum(top_part, axis=0), jnp.sum(low_part, axis=0))


def reference(entries, tile_cols, block_now, block_prev, block_prev2, gram_prev, square_prev, inverse_prev, inverse_prev2):
    col_tiles = TCOLS * N_COL
    slot_owner = (jnp.arange(SLOTS * N_COL, dtype=jnp.int32) // SLOTS) * TCOLS
    global_cols = (tile_cols + slot_owner[None, :]).astype(jnp.int32)

    def apply_operator(block):
        top_part, low_part = split_digits(block)
        digits = jnp.concatenate([top_part, low_part], axis=0).reshape(2 * BLOCK, col_tiles, TILE)

        def per_row(running, inputs):
            tile_row, cols_row = inputs
            matrix = tile_row.astype(jnp.float32)
            picked = jnp.take(digits, cols_row, axis=1)
            raw_sums = jnp.einsum('bsk,sjk->bj', picked, matrix, precision=lax.Precision.HIGHEST)
            projected = fold_digits(raw_sums[:BLOCK], raw_sums[BLOCK:])
            proj_top, proj_low = split_digits(projected)
            proj_digits = jnp.concatenate([proj_top, proj_low], axis=0)
            spread = jnp.einsum('bj,sjk->bsk', proj_digits, matrix, precision=lax.Precision.HIGHEST)
            per_slot = fold_digits(spread[:BLOCK], spread[BLOCK:])
            return residue(running.at[:, cols_row, :].add(per_slot)), None

        totals, unused = lax.scan(per_row, jnp.zeros((BLOCK, col_tiles, TILE), jnp.float32), (entries, global_cols))
        return totals.reshape(BLOCK, col_tiles * TILE)

    current = block_now.astype(jnp.float32)
    earlier = block_prev.astype(jnp.float32)
    earliest = block_prev2.astype(jnp.float32)
    gram_old = gram_prev.astype(jnp.float32)
    square_old = square_prev.astype(jnp.float32)
    inverse_old = inverse_prev.astype(jnp.float32)
    inverse_older = inverse_prev2.astype(jnp.float32)
    results = []
    for iteration in range(2):
        applied = apply_operator(current)
        gram_now = gram_whole(current, applied)
        square_now = gram_whole(applied, applied)
        inverse_now = inverse_matrix(gram_now)
        coeffs = coefficients(gram_now, square_now, inverse_now, inverse_old, inverse_older, gram_old, square_old)
        stacked = jnp.concatenate([current, earlier, earliest], axis=0)
        following = residue(applied + combine_blocks(coeffs, stacked))
        results.append(following / modulus)
        earliest, earlier, current = earlier, current, following
        inverse_older, inverse_old = inverse_old, inverse_now
        gram_old, square_old = gram_now, square_now
    return results[0], results[1]
```

```python
import functools

import jax
import jax.numpy as jnp
from jax import lax
from jax.experimental import pallas as pl
from jax.experimental.pallas import tpu as pltpu
from jax.sharding import PartitionSpec as P

modulus = 65521.0
reciprocal = 1.0 / 65521.0
MESH = pl.DeviceIdType.MESH
CHUNKS = 4
GATHER, PARTIAL, SCATTER, GRAM, SQUARE_ROW, SQUARE_COL = range(6)


def near(values):
    return values - jnp.floor(values * reciprocal + 0.5) * modulus


def whole(values):
    signed = near(values)
    return jnp.where(signed < 0.0, signed + modulus, signed)


def split(values):
    top = jnp.floor(values * (1.0 / 256.0) + 0.5)
    return top, values - top * 256.0


def digits(values):
    top, low = split(values)
    return jnp.concatenate([top, low], axis=0).astype(jnp.bfloat16)


def fold_two(top, low):
    return near(near(top) * 256.0 + low)


def fold_three(upper, middle, lower):
    return near(near(upper) * 15.0 + near(middle) * 256.0 + near(lower))


def mulmod(left, right):
    top, low = split(right)
    return near(near(left * top) * 256.0 + left * low)


def dot(left, right):
    return jnp.dot(left, right, preferred_element_type=jnp.float32)


def dot_t(left, right):
    return lax.dot_general(
        left, right, (((1,), (1,)), ((), ())), preferred_element_type=jnp.float32
    )


def product_parts(left, right):
    order = left.shape[0]
    left_digits = digits(left)
    right_top, right_low = split(right)
    with_top = dot(left_digits, right_top.astype(jnp.bfloat16))
    with_low = dot(left_digits, right_low.astype(jnp.bfloat16))
    return with_top[:order], with_top[order:] + with_low[:order], with_low[order:]


def small_product(left, right):
    return fold_three(*product_parts(left, right))


def gram_tiles(tiles):
    order = tiles[0].shape[0]
    total = None
    for tile in tiles:
        both = digits(tile)
        term = dot_t(both, both)
        total = term if total is None else total + term
    return fold_three(
        total[:order, :order],
        total[:order, order:] + total[order:, :order],
        total[order:, order:],
    )


def power_inverse(number):
    result = None
    square = number
    for position in range(16):
        if 65519 >> position & 1:
            result = square if result is None else mulmod(result, square)
        if position < 15:
            square = mulmod(square, square)
    return result


def identity_of(order):
    rows = lax.broadcasted_iota(jnp.int32, (order, order), 0)
    lanes = lax.broadcasted_iota(jnp.int32, (order, order), 1)
    return jnp.where(rows == lanes, 1.0, 0.0).astype(jnp.float32)


def inverse_of(matrix):
    order = matrix.shape[0]
    work = jnp.concatenate([matrix, identity_of(order)], axis=1)
    rows = lax.broadcasted_iota(jnp.int32, (order, 1), 0)
    for column in range(order):
        entry = work[:, column : column + 1]
        usable = (entry != 0.0) & (rows >= column)
        first = jnp.min(jnp.where(usable, rows, order), axis=0, keepdims=True)
        chosen = rows == jnp.where(first == order, column, first)
        pivot_row = jnp.sum(jnp.where(chosen, work, 0.0), axis=0, keepdims=True)
        pivot = jnp.sum(jnp.where(chosen, entry, 0.0), axis=0, keepdims=True)
        swapped = jnp.where(chosen, work[column : column + 1, :], work)
        factor = jnp.where(chosen, entry[column : column + 1, :], entry)
        pivot_row = jnp.where(pivot == 0.0, 0.0, pivot_row)
        pivot = jnp.where(pivot == 0.0, 1.0, pivot)
        pivot_top, pivot_low = split(pivot)
        factor_top, factor_low = split(factor)
        upper = near(pivot_top * swapped - factor_top * pivot_row)
        reduced = near(upper * 256.0 + (pivot_low * swapped - factor_low * pivot_row))
        work = jnp.where(rows == column, pivot_row, reduced)
    left = work[:, :order]
    diagonal = jnp.sum(left * identity_of(order), axis=1, keepdims=True)
    return mulmod(work[:, order:], power_inverse(diagonal))


def pack(values):
    rows = values.shape[0] // 4
    return jnp.concatenate([values[g * rows : (g + 1) * rows] for g in range(4)], axis=1)


def unpack(values):
    width = values.shape[1] // 4
    return jnp.concatenate([values[:, g * width : (g + 1) * width] for g in range(4)], axis=0)


def flipped(place, mask, count):
    assert count & (count - 1) == 0
    bit = 1
    moved = place
    while bit < count:
        if mask & bit:
            moved = moved + bit - 2 * bit * lax.rem(place // bit, 2)
        bit *= 2
    return moved


def kernel(
    n_row, n_col, chunks, plan, cols_any, entries_any, now_any, prev_any, prev2_any,
    gram_any, square_any, inverse_any, inverse2_any, next_ref, later_ref,
    cols_ref, entries_ref, blocks, smalls, tile16, full_a, full_b, partial, folded, running,
    outgoing, incoming, gram_buf, square_row, square_col, order_ref, begin_ref,
    local_sem, send_sem, recv_sem,
):
    my_row = lax.axis_index("row")
    my_col = lax.axis_index("col")
    tile_rows, slots, size = entries_ref.shape[:3]
    stored = tile_rows * slots
    order, width = blocks.shape[1:]
    rows = order // chunks
    share = width // size
    half = n_row // 2

    def row_peer(m):
        return flipped(my_row, m, n_row)

    def col_peer(m):
        return flipped(my_col, m, n_col)

    barrier = pltpu.get_barrier_semaphore()
    for m in range(1, n_row):
        pl.semaphore_signal(barrier, inc=1, device_id=(row_peer(m), my_col), device_id_type=MESH)
    for m in range(1, n_col):
        pl.semaphore_signal(barrier, inc=1, device_id=(my_row, col_peer(m)), device_id_type=MESH)

    inputs = [
        (now_any, blocks.at[0]), (cols_any, cols_ref), (entries_any, entries_ref),
        (gram_any, smalls.at[0]), (square_any, smalls.at[1]),
        (inverse_any, smalls.at[2]), (inverse2_any, smalls.at[3]),
        (prev_any, blocks.at[1]), (prev2_any, blocks.at[2]),
    ]
    loads = [
        pltpu.make_async_copy(source, target, local_sem.at[k])
        for k, (source, target) in enumerate(inputs)
    ]
    for copy in loads:
        copy.start()

    def sem_of(key):
        return plan.setdefault(key, len(plan))

    sent = {}

    def send(kind, key, source, target, device):
        sent[kind] = sent.get(kind, 0) + 1
        pltpu.make_async_remote_copy(
            src_ref=source, dst_ref=target,
            send_sem=send_sem.at[kind], recv_sem=recv_sem.at[sem_of(key)],
            device_id=device, device_id_type=MESH,
        ).start()

    def received(key, ref):
        pltpu.make_async_copy(ref, ref, recv_sem.at[sem_of(key)]).wait()

    def row_device(m):
        return (row_peer(m), my_col)

    def tiles_of(values):
        return [values[:, t * size : (t + 1) * size] for t in range(share)]

    def cut(values, c):
        return values[c * rows : (c + 1) * rows]

    def join(parts):
        return parts[0] if len(parts) == 1 else jnp.concatenate(parts, axis=0)

    def small(k):
        return near(smalls[k].astype(jnp.float32))

    identity = identity_of(order)

    def block(full, c, row):
        return full[c].at[pl.ds(row * share, share)]

    def gather_start(full, c):
        mine = block(full, c, my_row)
        send(GATHER, ("across", c), mine, mine, row_device(1))
        for m in range(1, half):
            send(GATHER, ("along", c, m), mine, mine, row_device(2 * m))

    def gather_relay(full, c):
        for m in range(1, half):
            got = block(full, c, row_peer(2 * m))
            received(("along", c, m), got)
            send(GATHER, ("across", c), got, got, row_device(1))

    def gather_finish(full, c):
        received(("across", c), full[c].at[pl.ds(0, half * share)])

    loads[0].wait()
    current = tiles_of(near(blocks[0].astype(jnp.float32)))
    for c in range(chunks):
        for t in range(share):
            full_a[c][my_row * share + t] = cut(current[t], c)
    pl.semaphore_wait(barrier, n_row + n_col - 2)
    for c in range(chunks):
        gather_start(full_a, c)

    loads[2].wait()
    for i in range(stored):
        tile16[i] = entries_ref[i // slots, i % slots].astype(jnp.float32).astype(jnp.bfloat16)
    loads[1].wait()
    cols = [cols_ref[i // slots, i % slots] for i in range(stored)]

    def as_int(flag):
        return jnp.where(flag, 1, 0).astype(jnp.int32)

    def sort_slots():
        ranks = []
        for i in range(stored):
            rank = jnp.int32(0)
            for j in range(stored):
                if j != i:
                    rank = rank + as_int(cols[j] <= cols[i] if j < i else cols[j] < cols[i])
            ranks.append(rank)
        for k in range(stored):
            place = jnp.int32(0)
            for i in range(1, stored):
                place = place + jnp.where(ranks[i] == k, i, 0).astype(jnp.int32)
            order_ref[k] = place

        def count(tile, carry):
            below = jnp.int32(0)
            for i in range(stored):
                below = below + as_int(cols[i] < tile)
            begin_ref[tile] = below
            return carry

        lax.fori_loop(0, n_row * share + 1, count, 0)

    for c in range(chunks):
        gather_relay(full_a, c)

    def forward(step, full, c):
        base = (step * chunks + c) * n_col
        for r in range(tile_rows):
            total = None
            for s in range(slots):
                picked = full[c][cols[r * slots + s]]
                term = dot_t(digits(picked), tile16[r * slots + s])
                total = term if total is None else total + term
            partial[base + my_col, :, r * size : (r + 1) * size] = fold_two(
                total[:rows], total[rows:]
            )
        own = partial.at[base + my_col]
        for m in range(1, n_col):
            send(PARTIAL, ("partial", step, c), own, own, (my_row, col_peer(m)))

    def summed_partial(step, c):
        base = (step * chunks + c) * n_col
        received(("partial", step, c), partial.at[pl.ds(base, n_col - 1)])
        total = partial[base]
        for k in range(1, n_col):
            total = total + partial[base + k]
        return [total[:, r * size : (r + 1) * size] for r in range(tile_rows)]

    def reduce_small(kind, key, buffer, base, count, place, value, devices):
        buffer[base + place] = value
        own = buffer.at[base + place]
        for device in devices:
            send(kind, key, own, own, device)

        def finish():
            received(key, buffer.at[pl.ds(base, count - 1)])
            total = buffer[base]
            for k in range(1, count):
                total = total + buffer[base + k]
            return near(total)

        return finish

    def gram_start(step, projected):
        return reduce_small(
            GRAM, ("gram",), gram_buf, step * n_row, n_row, my_row,
            pack(gram_tiles(projected)), [row_device(m) for m in range(1, n_row)],
        )

    def scatter_start(step, c, projected):
        for r in range(tile_rows):
            both = digits(projected[r])
            for s in range(slots):
                product = dot(both, tile16[r * slots + s])
                folded[c * stored + r * slots + s] = fold_two(product[:rows], product[rows:])
        total = jnp.zeros((rows, size), jnp.float32)
        first_sum = c * (stored + 1)
        running[first_sum] = total
        for i in range(stored):
            total = total + folded[c * stored + order_ref[i]]
            running[first_sum + i + 1] = total

        def finish_block(peer):
            for t in range(share):
                tile = peer * share + t
                outgoing[(step * chunks + c) * n_row + peer, :, t * size : (t + 1) * size] = (
                    running[first_sum + begin_ref[tile + 1]] - running[first_sum + begin_ref[tile]]
                )

        for m in range(half - 1, -1, -1):
            peer = row_peer(2 * m + 1)
            finish_block(peer)
            send(
                SCATTER, ("scatter", c, m), outgoing.at[(step * chunks + c) * n_row + peer],
                incoming.at[(step * chunks + c) * n_row + m], row_device(1),
            )
        for m in range(half - 1, -1, -1):
            finish_block(row_peer(2 * m))

    def scatter_relay(step, c):
        base = (step * chunks + c) * n_row
        for m in range(half - 1, 0, -1):
            got = incoming.at[base + m]
            received(("scatter", c, m), got)
            own = outgoing.at[base + row_peer(2 * m)]
            own[...] = own[...] + got[...]
            send(
                SCATTER, ("scattered", c), own, incoming.at[base + half + m], row_device(2 * m)
            )

    def scatter_finish(step, c):
        base = (step * chunks + c) * n_row
        received(("scatter", c, 0), incoming.at[base])
        received(("scattered", c), incoming.at[pl.ds(base + half + 1, half - 1)])
        total = outgoing[base + my_row] + incoming[base]
        for m in range(half + 1, n_row):
            total = total + incoming[base + m]
        return tiles_of(near(total))

    def square_start(step, applied):
        return reduce_small(
            SQUARE_ROW, ("square_row",), square_row, step * n_row, n_row, my_row,
            pack(gram_tiles(applied)), [row_device(m) for m in range(1, n_row)],
        )

    def square_pass(step, value):
        return reduce_small(
            SQUARE_COL, ("square_col", step), square_col, step * n_col, n_col, my_col,
            value, [(my_row, col_peer(m)) for m in range(1, n_col)],
        )

    def third_of(square_old, gram_old, inverse_old, inverse_older):
        middle = near(identity - small_product(inverse_old, gram_old))
        return -small_product(
            small_product(near(square_old + gram_old), middle), inverse_older
        )

    def parts_of(second, third, earlier, earliest):
        parts = []
        for t in range(share):
            one = product_parts(second, earlier[t])
            two = product_parts(third, earliest[t])
            upper, mid, lower = [a + b for a, b in zip(one, two)]
            parts.append(near(upper) * 15.0 + near(mid) * 256.0 + lower)
        return parts

    def advance(out, first, ready, current):
        following = []
        for t in range(share):
            upper, mid, lower = product_parts(first, current[t])
            value = whole(ready[t] + near(upper) * 15.0 + near(mid) * 256.0 + lower)
            out[:, t * size : (t + 1) * size] = value
            following.append(value)
        return following

    def joined(pieces):
        return [join([piece[k] for piece in pieces]) for k in range(len(pieces[0]))]

    for c in range(chunks):
        gather_finish(full_a, c)
        forward(0, full_a, c)
    sort_slots()
    for copy in loads[3:]:
        copy.wait()
    earlier = tiles_of(near(blocks[1].astype(jnp.float32)))
    earliest = tiles_of(near(blocks[2].astype(jnp.float32)))
    gram_old, square_old, inverse_old, inverse_older = [small(k) for k in range(4)]

    pieces = []
    for c in range(chunks):
        pieces.append([near(v) for v in summed_partial(0, c)])
        if c == chunks - 1:
            projected = joined(pieces)
            gram_finish = gram_start(0, projected)
        scatter_start(0, c, pieces[c])
    third = third_of(square_old, gram_old, inverse_old, inverse_older)
    for c in range(chunks):
        scatter_relay(0, c)
    gram_now = unpack(gram_finish())
    second = -small_product(gram_now, inverse_old)
    parts = parts_of(second, third, earlier, earliest)
    applied_pieces, ready_pieces = [], []
    for c in range(chunks):
        applied = scatter_finish(0, c)
        ready = [near(applied[t] + cut(parts[t], c)) for t in range(share)]
        for t in range(share):
            full_b[c][my_row * share + t] = ready[t]
        gather_start(full_b, c)
        applied_pieces.append(applied)
        ready_pieces.append(ready)
        if c == 0:
            inverse_now = inverse_of(gram_now)
    ready = joined(ready_pieces)
    square_finish = square_start(0, joined(applied_pieces))
    for c in range(chunks):
        gather_relay(full_b, c)
    square_finish = square_pass(0, square_finish())
    for c in range(chunks):
        gather_finish(full_b, c)
        forward(1, full_b, c)
    square_now = unpack(square_finish())
    first = near(identity - small_product(near(square_now + gram_now), inverse_now))
    rest = [fold_three(*product_parts(first, projected[r])) for r in range(tile_rows)]

    pieces = []
    for c in range(chunks):
        pieces.append(
            [near(v + cut(rest[r], c)) for r, v in enumerate(summed_partial(1, c))]
        )
        if c == chunks - 1:
            gram_finish = gram_start(1, joined(pieces))
        scatter_start(1, c, pieces[c])
    following = [near(v) for v in advance(next_ref, first, ready, current)]
    third = third_of(square_now, gram_now, inverse_now, inverse_old)
    for c in range(chunks):
        scatter_relay(1, c)
    gram_last = unpack(gram_finish())
    inverse_last = inverse_of(gram_last)
    second = -small_product(gram_last, inverse_now)
    parts = parts_of(second, third, current, earlier)
    applied = joined([scatter_finish(1, c) for c in range(chunks)])
    square_finish = square_start(1, applied)
    ready = [applied[t] + parts[t] for t in range(share)]
    square_finish = square_pass(1, square_finish())
    square_last = unpack(square_finish())
    first = near(identity - small_product(near(square_last + gram_last), inverse_last))
    advance(later_ref, first, [near(v) for v in ready], following)

    def all_sent(kind, ref):
        blocks_sent = ref.at[pl.ds(0, sent[kind])]
        pltpu.make_async_copy(blocks_sent, blocks_sent, send_sem.at[kind]).wait()

    all_sent(GATHER, outgoing)
    all_sent(SCATTER, outgoing)
    all_sent(PARTIAL, partial)
    all_sent(GRAM, gram_buf)
    all_sent(SQUARE_ROW, square_row)
    all_sent(SQUARE_COL, square_col)


def body(
    n_row, n_col, entries, tile_cols, block_now, block_prev, block_prev2,
    gram_prev, square_prev, inverse_prev, inverse_prev2,
):
    tile_rows, slots, size = entries.shape[:3]
    order, width = block_now.shape
    share = width // size
    col_tiles = n_row * share
    stored = tile_rows * slots
    half = n_row // 2
    chunks = CHUNKS
    rows = order // chunks
    assert tile_rows <= 4 and share <= 4 and n_row % 2 == 0 and rows % 8 == 0

    f32, i32 = jnp.float32, jnp.int32
    anywhere = pl.BlockSpec(memory_space=pl.ANY)
    vmem = pl.BlockSpec(memory_space=pltpu.VMEM)
    packed = (order // 4, order * 4)
    arrivals = chunks * (2 * half + 3) + 4
    following, later = pl.pallas_call(
        functools.partial(kernel, n_row, n_col, chunks, {}),
        out_shape=(jax.ShapeDtypeStruct((order, width), f32),) * 2,
        in_specs=[anywhere] * 9,
        out_specs=(vmem, vmem),
        scratch_shapes=[
            pltpu.SMEM(tile_cols.shape, i32),
            pltpu.VMEM(entries.shape, i32),
            pltpu.VMEM((3, order, width), i32),
            pltpu.VMEM((4, order, order), i32),
            pltpu.VMEM((stored, size, size), jnp.bfloat16),
            [pltpu.VMEM((col_tiles, rows, size), f32)] * chunks,
            [pltpu.VMEM((col_tiles, rows, size), f32)] * chunks,
            pltpu.VMEM((2 * chunks * n_col, rows, tile_rows * size), f32),
            pltpu.VMEM((chunks * stored, rows, size), f32),
            pltpu.VMEM((chunks * (stored + 1), rows, size), f32),
            pltpu.VMEM((2 * chunks * n_row, rows, width), f32),
            pltpu.VMEM((2 * chunks * n_row, rows, width), f32),
            pltpu.VMEM((2 * n_row,) + packed, f32),
            pltpu.VMEM((2 * n_row,) + packed, f32),
            pltpu.VMEM((2 * n_col,) + packed, f32),
            pltpu.SMEM((stored,), i32),
            pltpu.SMEM((col_tiles + 1,), i32),
            pltpu.SemaphoreType.DMA((9,)),
            pltpu.SemaphoreType.DMA((6,)),
            pltpu.SemaphoreType.DMA((arrivals,)),
        ],
        compiler_params=pltpu.CompilerParams(collective_id=0, has_side_effects=True),
    )(
        tile_cols, entries, block_now, block_prev, block_prev2,
        gram_prev, square_prev, inverse_prev, inverse_prev2,
    )
    return following / modulus, later / modulus


def solution(mesh):
    placed = (
        P("row", "col", None, None),
        P("row", "col"),
        P(None, ("col", "row")),
        P(None, ("col", "row")),
        P(None, ("col", "row")),
        P(),
        P(),
        P(),
        P(),
    )
    return jax.shard_map(
        functools.partial(body, mesh.shape["row"], mesh.shape["col"]),
        mesh=mesh,
        in_specs=placed,
        out_specs=(P(None, ("col", "row")), P(None, ("col", "row"))),
        check_vma=False,
    )
```
